32 devices in a mesh: dp: 2 (over x), cluster: 16 (over z, y, core).
Axes of the slice: x: 2, y: 2, z: 4, core: 2. Of those that a mesh axis runs over, the one named last changes fastest.
Arguments:
- queries: bfloat16 [4096, 768], P(('dp', 'cluster')), may hold values from -6 to 6
- shortlist: int32 [4096, 8], P(('dp', 'cluster')), may hold values from 0 to 15, all different within a row; in each aligned block of 128 rows (0 to 127, 128 to 255, ...) at most 128 rows name the same one
- positives: int32 [4096, 8], P(('dp', 'cluster')), may hold values from 0 to 255
- weights: bfloat16 [16, 256, 768], P('cluster'), may hold values from -0.21875 to 0.21875
- first_moment: float32 [16, 256, 768], P('cluster'), may hold values from -24 to 24
- second_moment: float32 [16, 256, 768], P('cluster'), may hold values from 0.5 to 50
Outputs:
- new_weights: bfloat16 [16, 256, 768], P('cluster')
- new_first: float32 [16, 256, 768], P('cluster')
- new_second: float32 [16, 256, 768], P('cluster')
- query_grad: bfloat16 [4096, 768], P(('dp', 'cluster'))
The draws below stay inside these ranges and needn't reach their ends.
Inputs may be any that keep to these rules, and one draw needn't show every extreme that they name: `shortlist`: each row names 8 different clusters. In the rows of one device no cluster is named by more than 128 rows, a bound that some block reaches of them.
All inputs are finite; a program needn't handle non-finite values.
Results may differ from the reference program's by a relative error of at most 0.0085.
Values may be sent and summed in bfloat16 or wider, within the bound.
No kernel may reach another device: no remote copies, remote signals or barrier semaphores. Data moves between devices by JAX's collectives and lax.ppermute only.
A program may use at most 64 MiB of HBM per device.

```python
import math
import jax
import jax.numpy as jnp
import numpy as np
from jax import lax

D = 768
LAB = 256
TOP = 8
QRY_DEV = 128
QUERIES = 4096
CLUSTERS = 16
MOST = 128


def place_ends(entries, own_key, low, largest):
    longest = entries.shape.index(max(entries.shape))
    spots = []
    for shift in (0, 1):
        where = [jax.random.randint(jax.random.fold_in(own_key, axis), (), 0, length) for axis, length in enumerate(entries.shape)]
        where[longest] = (where[longest] + shift) % entries.shape[longest]
        spots.append(tuple(where))
    return entries.at[spots[0]].set(low).at[spots[1]].set(largest)


def block_levels(own_key, dims, cuts, low, high):
    gain, own = 1.0, jax.random.fold_in(own_key, 6)
    for axis_at, blocks in cuts:
        steps = jnp.exp(jax.random.uniform(jax.random.fold_in(own, axis_at), (blocks,), jnp.float32, low / len(cuts), high / len(cuts)))
        gain = gain * jnp.repeat(steps, dims[axis_at] // blocks).reshape([-1 if axis == axis_at else 1 for axis in range(len(dims))])
    return gain


def shared_out(own_key, own, number, rows, number_of, top, limit, lean):
    order = jax.random.permutation(own_key, number_of)
    packed, common = load_shares(number_of, rows * top, limit, lean, True), load_shares(number_of, rows * top, limit, lean, False)
    places = jnp.arange(number_of)

    def named(lengths, offset_by):
        used = int((lengths > 0).sum())
        fixed = max(1, used // 4)
        passed = fixed + (places - fixed + offset_by * (used - fixed)) % max(1, number_of - fixed)
        return jnp.zeros((number_of,), jnp.int32).at[order[jnp.where(places < fixed, places, passed)]].set(jnp.asarray(lengths, jnp.int32))

    lengths = jnp.where(number % 4 == 0, named(packed, number // 4), named(common, number - number // 4 - 1))
    mixed = jax.random.permutation(jax.random.fold_in(own, 3), number_of)
    donor, taker = mixed[0:number_of // 2 * 2:2], mixed[1:number_of // 2 * 2:2]
    margin = jnp.minimum(lengths[donor] - 1, limit - lengths[taker]) // 2
    margin = jnp.where((donor == order[0]) | (taker == order[0]) | (lengths[taker] == 0), 0, jnp.maximum(margin, 0))
    passed = jax.random.randint(jax.random.fold_in(own, 4), (number_of // 2,), 0, 1 << 20) % (margin + 1)
    lengths = lengths.at[donor].add(-passed).at[taker].add(passed)
    items = jnp.searchsorted(jnp.cumsum(lengths), jnp.arange(rows * top), side="right").astype(jnp.int32)
    grid = items.reshape(top, rows).T
    grid = grid[jax.random.permutation(jax.random.fold_in(own, 1), rows)]
    offset_by = jax.random.randint(jax.random.fold_in(own, 2), (rows, 1), 0, top)
    return jnp.take_along_axis(grid, (jnp.arange(top)[None, :] + offset_by) % top, axis=1)


def load_shares(amount, total, limit, skew, full):
    portions = [(1 << 20) // math.isqrt(standing ** skew) + 1 for standing in range(1, amount + 1)]
    largest = limit if full else min(limit, max(-(-total // amount), total * portions[0] // sum(portions)))
    least = 1 if total - largest >= amount - 1 else 0
    counts, surplus = [largest] + [least] * (amount - 1), total - largest - least * (amount - 1)
    while surplus > 0:
        free = [i for i in range(1, amount) if counts[i] < largest] or [i for i in range(1, amount) if counts[i] < limit]
        whole, remaining = sum([portions[i] for i in free]), surplus
        for i in free:
            extra = min(limit - counts[i], max(1, remaining * portions[i] // whole), surplus)
            counts[i] = counts[i] + extra
            surplus = surplus - extra
    return np.array(counts)


def gaussian(own_key, dims, width, bound, pieces=(), kind=jnp.bfloat16):
    drawn = width * jax.random.normal(own_key, dims, jnp.float32)
    if pieces:
        drawn = drawn * block_levels(own_key, dims, pieces, -0.22, 0.18)
    return jnp.clip(drawn, -bound, bound).astype(kind)


def setup_inputs(seed: int = 0) -> dict:
    splits = jax.random.split(jax.random.key(seed), 7)
    queries = gaussian(splits[0], (QUERIES, D), 1.0, 6.0, ((0, 32),))
    shortlist_keys = jax.random.split(jax.random.fold_in(splits[1], 1), QUERIES // QRY_DEV)
    shortlist_turns = jax.random.permutation(jax.random.fold_in(splits[1], 3), QUERIES // QRY_DEV)
    shortlist = jax.vmap(lambda own, number: shared_out(jax.random.fold_in(splits[1], 2), own, number, QRY_DEV, CLUSTERS, TOP, MOST, 2))(shortlist_keys, shortlist_turns).reshape((QUERIES, TOP))
    positives = place_ends(jax.random.randint(splits[2], (QUERIES, TOP), 0, LAB), jax.random.fold_in(splits[2], 1), 0, LAB - 1).astype(jnp.int32)
    weights = gaussian(splits[3], (CLUSTERS, LAB, D), D ** -0.5, 0.21875, ((0, 16),))
    first_moment = gaussian(splits[4], (CLUSTERS, LAB, D), 4.0, 24.0, ((0, 16),), jnp.float32)
    second_moment = jnp.clip(jnp.exp(math.log(50.0) - 4.6051702 * jax.random.uniform(splits[5], (CLUSTERS, LAB, D), jnp.float32) ** block_levels(splits[5], (CLUSTERS, LAB, D), ((0, 16),), -0.2, 0.2)), 0.5, 50.0)
    return {"queries": queries, "shortlist": shortlist, "positives": positives, "weights": weights, "first_moment": first_moment, "second_moment": second_moment}


beta_one = 0.9
beta_two = 0.999
learn_rate = 0.01
adam_eps = 1e-08
adam_step = 10.0

def adam_update(cluster_weights, first_moment, second_moment, gradient):
    first_new = beta_one * first_moment + (1.0 - beta_one) * gradient
    second_new = beta_two * second_moment + (1.0 - beta_two) * gradient * gradient
    first_hat = first_new / (1.0 - beta_one ** adam_step)
    second_hat = second_new / (1.0 - beta_two ** adam_step)
    stepped = cluster_weights.astype(jnp.float32) - learn_rate * first_hat / (jnp.sqrt(second_hat) + adam_eps)
    return (stepped.astype(jnp.bfloat16), first_new, second_new)

def reference(queries, shortlist, positives, weights, first_moment, second_moment):
    fanout = shortlist.shape[1]
    visits = shortlist.reshape(-1).astype(jnp.int32)
    labels = positives.reshape(-1).astype(jnp.int32)
    capacity = QUERIES // QRY_DEV * MOST
    label_ids = jnp.arange(LAB, dtype=jnp.int32)
    slot_ids = jnp.arange(capacity, dtype=jnp.int32)

    def per_cluster(running, cluster):
        hits = visits == cluster
        picked = jnp.nonzero(hits, size=capacity, fill_value=0)[0].astype(jnp.int32)
        counted = jnp.sum(hits.astype(jnp.int32))
        in_use = slot_ids < counted
        query_rows = picked // fanout
        rows = jnp.where(in_use[:, None], queries[query_rows], jnp.zeros((), queries.dtype))
        lab_ids = jnp.where(in_use, labels[picked], -1)
        cluster_rows = lax.dynamic_index_in_dim(weights, cluster, 0, keepdims=False)
        scores = lax.dot_general(rows, cluster_rows, (((1,), (1,)), ((), ())), preferred_element_type=jnp.float32)
        target = (lab_ids[:, None] == label_ids[None, :]).astype(jnp.float32)
        coefficient = (jax.nn.sigmoid(scores) - target).astype(jnp.bfloat16)
        gradient = lax.dot_general(coefficient, rows, (((0,), (0,)), ((), ())), preferred_element_type=jnp.float32)
        visit_grad = jnp.dot(coefficient, cluster_rows, preferred_element_type=jnp.float32).astype(jnp.bfloat16)
        visit_grad = lax.optimization_barrier(visit_grad).astype(jnp.float32)
        running = running.at[query_rows].add(jnp.where(in_use[:, None], visit_grad, 0.0))
        return (running, gradient)
    running, gradients = lax.scan(per_cluster, jnp.zeros(queries.shape, jnp.float32), jnp.arange(CLUSTERS, dtype=jnp.int32))
    new_weights, new_first, new_second = adam_update(weights, first_moment, second_moment, gradients)
    return (new_weights, new_first, new_second, running.astype(jnp.bfloat16))
```

```python
import functools

import jax
import jax.numpy as jnp
from jax import lax
from jax.experimental import pallas as pl
from jax.experimental.pallas import tpu as pltpu
from jax.sharding import PartitionSpec as P


beta_one = 0.9
beta_two = 0.999
learn_rate = 0.01
adam_eps = 1e-08
adam_step = 10.0

NEAR = 4


def adam_update(cluster_weights, first_moment, second_moment, gradient):
    first_new = beta_one * first_moment + (1.0 - beta_one) * gradient
    second_new = beta_two * second_moment + (1.0 - beta_two) * gradient * gradient
    first_hat = first_new / (1.0 - beta_one**adam_step)
    second_hat = second_new / (1.0 - beta_two**adam_step)
    stepped = cluster_weights.astype(jnp.float32) - learn_rate * first_hat / (
        jnp.sqrt(second_hat) + adam_eps
    )
    return (stepped.astype(jnp.bfloat16), first_new, second_new)


def block_kernel(base_ref, q_ref, meta_ref, *refs):
    weight_refs, (out_ref, coef_ref) = refs[:NEAR], refs[NEAR:]
    fanout = meta_ref.shape[0] // 2
    labels, rows = weight_refs[0].shape[0], q_ref.shape[0]
    q = q_ref[...]
    listed, positive = meta_ref[:fanout, :], meta_ref[fanout:, :]
    label_ids = lax.broadcasted_iota(jnp.int32, (labels, rows), 0)
    total = jnp.zeros(out_ref.shape, jnp.float32)
    for j in range(NEAR):
        w = weight_refs[j][...]
        cluster = jnp.bitwise_xor(base_ref[0], j)
        code = jnp.max(jnp.where(listed == cluster, positive, -1), axis=0, keepdims=True)
        scores = lax.dot_general(
            w, q, (((1,), (1,)), ((), ())), preferred_element_type=jnp.float32
        )
        target = (label_ids == code).astype(jnp.float32)
        coef = jnp.where(code >= 0, jax.nn.sigmoid(scores) - target, 0.0).astype(jnp.bfloat16)
        coef_ref[j * labels : (j + 1) * labels, :] = coef
        total = total + lax.dot_general(
            coef, w, (((0,), (0,)), ((), ())), preferred_element_type=jnp.float32
        )
    out_ref[...] = total.astype(out_ref.dtype)


def block_work(base, q, meta, near_weights, out_dtype):
    rows, dim = q.shape
    labels = near_weights[0].shape[0]
    vmem = pl.BlockSpec(memory_space=pltpu.VMEM)
    flops = 4 * rows * labels * NEAR * dim
    return pl.pallas_call(
        block_kernel,
        out_shape=(
            jax.ShapeDtypeStruct((rows, dim), out_dtype),
            jax.ShapeDtypeStruct((NEAR * labels, rows), jnp.bfloat16),
        ),
        in_specs=[pl.BlockSpec(memory_space=pltpu.SMEM)] + [vmem] * (2 + NEAR),
        out_specs=(vmem, vmem),
        cost_estimate=pl.CostEstimate(
            flops=flops, bytes_accessed=4 * rows * dim, transcendentals=rows * labels * NEAR
        ),
        name="block",
    )(base, q, meta, *near_weights)


def grad_kernel(*refs):
    coef_refs, q_refs = refs[:NEAR], refs[NEAR : 2 * NEAR]
    own_ref, beside_ref, send_ref = refs[2 * NEAR :]
    labels = own_ref.shape[0]
    q = jnp.concatenate([ref[...] for ref in q_refs], axis=0)

    def part(j):
        coef = jnp.concatenate([r[j * labels : (j + 1) * labels, :] for r in coef_refs], axis=1)
        return jnp.dot(coef, q, preferred_element_type=jnp.float32)

    send_ref[:labels, :] = part(1).astype(jnp.bfloat16)
    send_ref[labels:, :] = part(3).astype(jnp.bfloat16)
    own_ref[...] = part(0)
    beside_ref[...] = part(2)


def grad_work(coefs, qs, labels):
    rows, dim = qs[0].shape
    vmem = pl.BlockSpec(memory_space=pltpu.VMEM)
    return pl.pallas_call(
        grad_kernel,
        out_shape=(
            jax.ShapeDtypeStruct((labels, dim), jnp.float32),
            jax.ShapeDtypeStruct((labels, dim), jnp.float32),
            jax.ShapeDtypeStruct((2 * labels, dim), jnp.bfloat16),
        ),
        in_specs=[vmem] * (2 * NEAR),
        out_specs=(vmem, vmem, vmem),
        cost_estimate=pl.CostEstimate(
            flops=2 * rows * NEAR * labels * NEAR * dim,
            bytes_accessed=4 * rows * dim,
            transcendentals=0,
        ),
        name="grad",
    )(*coefs, *qs)


def near_device(queries, shortlist, positives, weights, first_moment, second_moment):
    owners = lax.axis_size("cluster")
    lines = owners // NEAR
    labels = weights.shape[1]
    half = labels // 2
    base = lax.axis_index("cluster").astype(jnp.int32).reshape(1)

    def over_cluster(x, bits):
        return lax.ppermute(x, "cluster", [(i, i ^ bits) for i in range(owners)])

    def over_dp(x):
        return lax.ppermute(x, "dp", [(0, 1), (1, 0)])

    own_weights = weights[0]
    meta = jnp.concatenate([shortlist.T, positives.T], axis=0)
    metas = [meta] + [over_cluster(meta, NEAR * s) for s in range(1, lines)]
    qs = [queries] + [over_cluster(queries, NEAR * s) for s in range(1, lines)]
    beside = over_cluster(own_weights, 2)
    near_weights = [own_weights, over_cluster(own_weights, 1), beside, over_cluster(beside, 1)]

    outs, coefs = [], []
    for s in range(lines):
        out, coef = block_work(
            base, qs[s], metas[s], near_weights, jnp.float32 if s == 0 else jnp.bfloat16
        )
        outs.append(out)
        coefs.append(coef)
    total = outs[0]
    for s in range(1, lines):
        total = total + over_cluster(outs[s], NEAR * s).astype(jnp.float32)
    query_grad = total.astype(jnp.bfloat16)

    own, near, send = grad_work(coefs, qs, labels)
    got = over_cluster(send, 1).astype(jnp.float32)
    own = own + got[:labels]
    near = near + got[labels:]
    top_near = near[:half].astype(jnp.bfloat16)
    low = jnp.concatenate([own[half:], near[half:]], axis=0).astype(jnp.bfloat16)
    got_top = over_cluster(top_near, 2).astype(jnp.float32)
    got_low = over_dp(low).astype(jnp.float32)
    top = (own[:half] + got_top).astype(jnp.bfloat16)
    low = low.astype(jnp.float32) + got_low
    low_own, low_near = low[:half], low[half:].astype(jnp.bfloat16)
    top = top.astype(jnp.float32) + over_dp(top).astype(jnp.float32)
    low_own = low_own + over_cluster(low_near, 2).astype(jnp.float32)
    gradient = jnp.concatenate([top, low_own], axis=0)
    new_weights, new_first, new_second = adam_update(
        own_weights, first_moment[0], second_moment[0], gradient
    )
    return (new_weights[None], new_first[None], new_second[None], query_grad)


def owner_work(arrived_rows, arrived_labels, cluster_rows):
    label_ids = jnp.arange(cluster_rows.shape[0], dtype=jnp.int32)
    scores = lax.dot_general(
        arrived_rows, cluster_rows, (((1,), (1,)), ((), ())), preferred_element_type=jnp.float32
    )
    target = (arrived_labels[:, None] == label_ids[None, :]).astype(jnp.float32)
    coefficient = (jax.nn.sigmoid(scores) - target).astype(jnp.bfloat16)
    gradient = lax.dot_general(
        coefficient, arrived_rows, (((0,), (0,)), ((), ())), preferred_element_type=jnp.float32
    )
    visit_grad = jnp.dot(coefficient, cluster_rows, preferred_element_type=jnp.float32).astype(
        jnp.bfloat16
    )
    return (gradient, visit_grad)


def dispatch_device(queries, shortlist, positives, weights, first_moment, second_moment):
    owners = lax.axis_size("cluster")
    rows_dev, fanout = shortlist.shape
    feature_dim = queries.shape[1]
    capacity = min(rows_dev, 2 * rows_dev * fanout // owners)
    visits = shortlist.reshape(-1)
    labels = positives.reshape(-1)
    onehot = (visits[:, None] == jnp.arange(owners, dtype=jnp.int32)[None, :]).astype(jnp.int32)
    visit_rank = jnp.sum((jnp.cumsum(onehot, axis=0) - onehot) * onehot, axis=1)
    slot_index = visits * capacity + visit_rank
    slot_visit = (
        jnp.full((owners * capacity,), -1, jnp.int32)
        .at[slot_index]
        .set(jnp.arange(visits.shape[0], dtype=jnp.int32))
    )
    filled = slot_visit >= 0
    clamped = jnp.maximum(slot_visit, 0)
    send_rows = jnp.where(filled[:, None], queries[clamped // fanout], jnp.zeros((), queries.dtype))
    send_labels = jnp.where(filled, labels[clamped], -1)
    cluster_rows = weights[0]
    exchange = functools.partial(
        lax.all_to_all, axis_name="cluster", split_axis=0, concat_axis=0, tiled=True
    )
    arrived_rows = exchange(send_rows.reshape(owners, capacity, feature_dim))
    arrived_labels = exchange(send_labels.reshape(owners, capacity))
    gradient, visit_grad = owner_work(
        arrived_rows.reshape(-1, feature_dim), arrived_labels.reshape(-1), cluster_rows
    )
    returned = exchange(visit_grad.reshape(owners, capacity, feature_dim))
    per_visit = returned.reshape(-1, feature_dim)[slot_index].astype(jnp.float32)
    query_grad = jnp.sum(per_visit.reshape(rows_dev, fanout, feature_dim), axis=1).astype(
        jnp.bfloat16
    )
    summed = lax.psum(gradient.astype(jnp.bfloat16), "dp").astype(jnp.float32)
    new_weights, new_first, new_second = adam_update(
        cluster_rows, first_moment[0], second_moment[0], summed
    )
    return (new_weights[None], new_first[None], new_second[None], query_grad)


def on_device(queries, shortlist, *rest):
    owners, copies = lax.axis_size("cluster"), lax.axis_size("dp")
    rows_dev, fanout = shortlist.shape
    dense = 2 * fanout >= owners and owners == NEAR * NEAR and copies == 2
    step = near_device if dense else dispatch_device
    return step(queries, shortlist, *rest)


def solution(mesh):
    split = P(("dp", "cluster"), None)
    owned = P("cluster", None, None)
    return jax.shard_map(
        on_device,
        mesh=mesh,
        in_specs=(split, split, split, owned, owned, owned),
        out_specs=(owned, owned, owned, split),
        check_vma=False,
    )
```

```python
import functools

import jax
import jax.numpy as jnp
from jax import lax
from jax.experimental import pallas as pl
from jax.experimental.pallas import tpu as pltpu
from jax.sharding import PartitionSpec as P


beta_one = 0.9
beta_two = 0.999
learn_rate = 0.01
adam_eps = 1e-08
adam_step = 10.0

NEAR = 4
KERNEL_VMEM = 16 << 20


def adam_update(cluster_weights, first_moment, second_moment, gradient):
    first_new = beta_one * first_moment + (1.0 - beta_one) * gradient
    second_new = beta_two * second_moment + (1.0 - beta_two) * gradient * gradient
    first_hat = first_new / (1.0 - beta_one**adam_step)
    second_hat = second_new / (1.0 - beta_two**adam_step)
    stepped = cluster_weights.astype(jnp.float32) - learn_rate * first_hat / (
        jnp.sqrt(second_hat) + adam_eps
    )
    return (stepped.astype(jnp.bfloat16), first_new, second_new)


def tn_dot(a, b):
    return lax.dot_general(a, b, (((0,), (0,)), ((), ())), preferred_element_type=jnp.float32)


def nt_dot(a, b):
    return lax.dot_general(a, b, (((1,), (1,)), ((), ())), preferred_element_type=jnp.float32)


def kernel_call(kernel, outs, args, flops):
    vmem = pl.BlockSpec(memory_space=pltpu.VMEM)
    specs = [pl.BlockSpec(memory_space=pltpu.SMEM)] + [vmem] * (len(args) - 1)
    return pl.pallas_call(
        kernel,
        out_shape=tuple(jax.ShapeDtypeStruct(shape, kind) for shape, kind in outs),
        in_specs=specs,
        out_specs=tuple([vmem] * len(outs)),
        compiler_params=pltpu.CompilerParams(vmem_limit_bytes=KERNEL_VMEM),
        cost_estimate=pl.CostEstimate(flops=flops, bytes_accessed=1 << 20, transcendentals=0),
    )(*args)


def coefficients(weights, q, listed, positive, cluster):
    labels, rows = weights.shape[0], q.shape[0]
    code = jnp.max(jnp.where(listed == cluster, positive, -1.0), axis=0, keepdims=True)
    label_ids = lax.broadcasted_iota(jnp.int32, (labels, rows), 0)
    target = (label_ids == code.astype(jnp.int32)).astype(jnp.float32)
    coef = jax.nn.sigmoid(nt_dot(weights, q)) - target
    return jnp.where(code >= 0.0, coef, 0.0).astype(jnp.bfloat16)


def unpack(packed_refs, rows, fanout):
    spare = [ref[rows : rows + fanout, :].astype(jnp.float32) for ref in packed_refs]
    q = jnp.concatenate([ref[:rows, :] for ref in packed_refs], axis=0)
    listed = jnp.concatenate([x[:, :rows] for x in spare], axis=1)
    positive = jnp.concatenate([x[:, rows : 2 * rows] for x in spare], axis=1)
    return q, listed, positive


def pack_kernel(base_ref, q_ref, listed_ref, positive_ref, out_ref):
    rows, dim = q_ref.shape
    fanout = listed_ref.shape[0]
    out_ref[:rows, :] = q_ref[...]
    ints = [listed_ref[...], positive_ref[...]]
    if dim > 2 * rows:
        ints.append(jnp.zeros((fanout, dim - 2 * rows), jnp.int32))
    spare = jnp.concatenate(ints, axis=1)
    out_ref[rows:, :] = spare.astype(jnp.float32).astype(jnp.bfloat16)


def own_kernel(rows, base_ref, packed_ref, *refs):
    weight_refs, (out_ref, coef_ref) = refs[:NEAR], refs[NEAR:]
    labels = weight_refs[0].shape[0]
    q, listed, positive = unpack([packed_ref], rows, packed_ref.shape[0] - rows)
    total = jnp.zeros(out_ref.shape, jnp.float32)
    for j in range(NEAR):
        w = weight_refs[j][...]
        cluster = jnp.bitwise_xor(base_ref[0], j).astype(jnp.float32)
        coef = coefficients(w, q, listed, positive, cluster)
        coef_ref[j * labels : (j + 1) * labels, :] = coef
        total = total + tn_dot(coef, w)
    out_ref[...] = total


def grad_kernel(rows, base_ref, own_coef_ref, *refs):
    packed_refs, weight_refs = refs[:NEAR], refs[NEAR : 2 * NEAR]
    coef_ref, send_ref, own_ref, beside_ref = refs[2 * NEAR :]
    labels = weight_refs[0].shape[0]
    fanout = packed_refs[0].shape[0] - rows
    q, listed, positive = unpack(packed_refs[1:], rows, fanout)
    own_q = packed_refs[0][:rows, :]

    def part(j):
        cluster = jnp.bitwise_xor(base_ref[0], j).astype(jnp.float32)
        coef = coefficients(weight_refs[j][...], q, listed, positive, cluster)
        spot = slice(j * labels, (j + 1) * labels)
        coef_ref[spot, :] = coef
        return jnp.dot(coef, q, preferred_element_type=jnp.float32) + jnp.dot(
            own_coef_ref[spot, :], own_q, preferred_element_type=jnp.float32
        )

    send_ref[:labels, :] = part(1).astype(jnp.bfloat16)
    send_ref[labels:, :] = part(3).astype(jnp.bfloat16)
    own_ref[...] = part(0)
    beside_ref[...] = part(2)


def back_kernel(rows, base_ref, coef_ref, *refs):
    weight_refs, out_refs = refs[:NEAR], refs[NEAR:]
    labels = weight_refs[0].shape[0]
    total = jnp.zeros((coef_ref.shape[1], weight_refs[0].shape[1]), jnp.float32)
    for j in range(NEAR):
        total = total + tn_dot(coef_ref[j * labels : (j + 1) * labels, :], weight_refs[j][...])
    for s, out_ref in enumerate(out_refs):
        out_ref[...] = total[s * rows : (s + 1) * rows, :].astype(jnp.bfloat16)


def near_device(queries, shortlist, positives, weights, first_moment, second_moment):
    owners = lax.axis_size("cluster")
    lines = owners // NEAR
    rows, fanout = shortlist.shape
    labels, dim = weights.shape[1:]
    half = labels // 2
    others = (lines - 1) * rows
    base = lax.axis_index("cluster").astype(jnp.int32).reshape(1)
    low_type, wide = jnp.bfloat16, jnp.float32

    def over_cluster(x, bits):
        return lax.ppermute(x, "cluster", [(i, i ^ bits) for i in range(owners)])

    def over_dp(x):
        return lax.ppermute(x, "dp", [(0, 1), (1, 0)])

    own_weights = weights[0]
    (packed,) = kernel_call(
        pack_kernel,
        [((rows + fanout, dim), low_type)],
        [base, queries, shortlist.T, positives.T],
        0,
    )
    packs = [packed] + [over_cluster(packed, NEAR * s) for s in range(1, lines)]
    weight_core = over_cluster(own_weights, 1)
    beside = over_cluster(own_weights, 2)
    near_weights = [own_weights, weight_core, beside, over_cluster(beside, 1)]

    total, own_coef = kernel_call(
        functools.partial(own_kernel, rows),
        [((rows, dim), wide), ((NEAR * labels, rows), low_type)],
        [base, packed, *near_weights],
        4 * rows * NEAR * labels * dim,
    )
    coef, send, own, near = kernel_call(
        functools.partial(grad_kernel, rows),
        [
            ((NEAR * labels, others), low_type),
            ((2 * labels, dim), low_type),
            ((labels, dim), wide),
            ((labels, dim), wide),
        ],
        [base, own_coef, *packs, *near_weights],
        4 * others * NEAR * labels * dim,
    )
    got = over_cluster(send, 1).astype(wide)
    backs = kernel_call(
        functools.partial(back_kernel, rows),
        [((rows, dim), low_type)] * (lines - 1),
        [base, coef, *near_weights],
        2 * others * NEAR * labels * dim,
    )
    for s in range(1, lines):
        total = total + over_cluster(backs[s - 1], NEAR * s).astype(wide)
    query_grad = total.astype(low_type)

    own = own + got[:labels]
    near = near + got[labels:]
    low = jnp.concatenate([own[half:], near[half:]], axis=0).astype(low_type)
    got_top = over_cluster(near[:half].astype(low_type), 2).astype(wide)
    got_low = over_dp(low).astype(wide)
    top = (own[:half] + got_top).astype(low_type)
    low = low.astype(wide) + got_low
    top = top.astype(wide) + over_dp(top).astype(wide)
    low_own = low[:half] + over_cluster(low[half:].astype(low_type), 2).astype(wide)
    gradient = jnp.concatenate([top, low_own], axis=0)
    new_weights, new_first, new_second = adam_update(
        own_weights, first_moment[0], second_moment[0], gradient
    )
    return (new_weights[None], new_first[None], new_second[None], query_grad)


def owner_work(arrived_rows, arrived_labels, cluster_rows):
    label_ids = jnp.arange(cluster_rows.shape[0], dtype=jnp.int32)
    scores = lax.dot_general(
        arrived_rows, cluster_rows, (((1,), (1,)), ((), ())), preferred_element_type=jnp.float32
    )
    target = (arrived_labels[:, None] == label_ids[None, :]).astype(jnp.float32)
    coefficient = (jax.nn.sigmoid(scores) - target).astype(jnp.bfloat16)
    gradient = lax.dot_general(
        coefficient, arrived_rows, (((0,), (0,)), ((), ())), preferred_element_type=jnp.float32
    )
    visit_grad = jnp.dot(coefficient, cluster_rows, preferred_element_type=jnp.float32).astype(
        jnp.bfloat16
    )
    return (gradient, visit_grad)


def dispatch_device(queries, shortlist, positives, weights, first_moment, second_moment):
    owners = lax.axis_size("cluster")
    rows_dev, fanout = shortlist.shape
    feature_dim = queries.shape[1]
    capacity = min(rows_dev, 2 * rows_dev * fanout // owners)
    visits = shortlist.reshape(-1)
    labels = positives.reshape(-1)
    onehot = (visits[:, None] == jnp.arange(owners, dtype=jnp.int32)[None, :]).astype(jnp.int32)
    visit_rank = jnp.sum((jnp.cumsum(onehot, axis=0) - onehot) * onehot, axis=1)
    slot_index = visits * capacity + visit_rank
    slot_visit = (
        jnp.full((owners * capacity,), -1, jnp.int32)
        .at[slot_index]
        .set(jnp.arange(visits.shape[0], dtype=jnp.int32))
    )
    filled = slot_visit >= 0
    clamped = jnp.maximum(slot_visit, 0)
    send_rows = jnp.where(filled[:, None], queries[clamped // fanout], jnp.zeros((), queries.dtype))
    send_labels = jnp.where(filled, labels[clamped], -1)
    cluster_rows = weights[0]
    exchange = functools.partial(
        lax.all_to_all, axis_name="cluster", split_axis=0, concat_axis=0, tiled=True
    )
    arrived_rows = exchange(send_rows.reshape(owners, capacity, feature_dim))
    arrived_labels = exchange(send_labels.reshape(owners, capacity))
    gradient, visit_grad = owner_work(
        arrived_rows.reshape(-1, feature_dim), arrived_labels.reshape(-1), cluster_rows
    )
    returned = exchange(visit_grad.reshape(owners, capacity, feature_dim))
    per_visit = returned.reshape(-1, feature_dim)[slot_index].astype(jnp.float32)
    query_grad = jnp.sum(per_visit.reshape(rows_dev, fanout, feature_dim), axis=1).astype(
        jnp.bfloat16
    )
    summed = lax.psum(gradient.astype(jnp.bfloat16), "dp").astype(jnp.float32)
    new_weights, new_first, new_second = adam_update(
        cluster_rows, first_moment[0], second_moment[0], summed
    )
    return (new_weights[None], new_first[None], new_second[None], query_grad)


def on_device(queries, shortlist, *rest):
    owners, copies = lax.axis_size("cluster"), lax.axis_size("dp")
    rows_dev, fanout = shortlist.shape
    dense = 2 * fanout >= owners and owners == NEAR * NEAR and copies == 2
    dense = dense and rest[1].shape[1] <= 256 and queries.shape[1] >= 2 * rows_dev
    step = near_device if dense else dispatch_device
    return step(queries, shortlist, *rest)


def solution(mesh):
    split = P(("dp", "cluster"), None)
    owned = P("cluster", None, None)
    return jax.shard_map(
        on_device,
        mesh=mesh,
        in_specs=(split, split, split, owned, owned, owned),
        out_specs=(owned, owned, owned, split),
        check_vma=False,
    )
```

```python
import functools

import jax
import jax.numpy as jnp
from jax import lax
from jax.experimental import pallas as pl
from jax.experimental.pallas import tpu as pltpu
from jax.sharding import PartitionSpec as P


beta_one = 0.9
beta_two = 0.999
learn_rate = 0.01
adam_eps = 1e-08
adam_step = 10.0

NEAR = 4
KERNEL_VMEM = 16 << 20


def adam_update(cluster_weights, first_moment, second_moment, gradient):
    first_new = beta_one * first_moment + (1.0 - beta_one) * gradient
    second_new = beta_two * second_moment + (1.0 - beta_two) * gradient * gradient
    first_hat = first_new / (1.0 - beta_one**adam_step)
    second_hat = second_new / (1.0 - beta_two**adam_step)
    stepped = cluster_weights.astype(jnp.float32) - learn_rate * first_hat / (
        jnp.sqrt(second_hat) + adam_eps
    )
    return (stepped.astype(jnp.bfloat16), first_new, second_new)


def tn_dot(a, b):
    return lax.dot_general(a, b, (((0,), (0,)), ((), ())), preferred_element_type=jnp.float32)


def nt_dot(a, b):
    return lax.dot_general(a, b, (((1,), (1,)), ((), ())), preferred_element_type=jnp.float32)


def kernel_call(kernel, outs, args, flops):
    vmem = pl.BlockSpec(memory_space=pltpu.VMEM)
    specs = [pl.BlockSpec(memory_space=pltpu.SMEM)] + [vmem] * (len(args) - 1)
    return pl.pallas_call(
        kernel,
        out_shape=tuple(jax.ShapeDtypeStruct(shape, kind) for shape, kind in outs),
        in_specs=specs,
        out_specs=tuple([vmem] * len(outs)),
        compiler_params=pltpu.CompilerParams(vmem_limit_bytes=KERNEL_VMEM),
        cost_estimate=pl.CostEstimate(flops=flops, bytes_accessed=1 << 20, transcendentals=0),
    )(*args)


def coefficients(weights, q, listed, positive, cluster):
    labels, rows = weights.shape[0], q.shape[0]
    code = jnp.max(jnp.where(listed == cluster, positive, -1.0), axis=0, keepdims=True)
    label_ids = lax.broadcasted_iota(jnp.int32, (labels, rows), 0)
    target = (label_ids == code.astype(jnp.int32)).astype(jnp.float32)
    coef = jax.nn.sigmoid(nt_dot(weights, q)) - target
    return jnp.where(code >= 0.0, coef, 0.0).astype(jnp.bfloat16)


def unpack(packed_refs, rows):
    spare = [ref[rows:, :].astype(jnp.float32) for ref in packed_refs]
    q = jnp.concatenate([ref[:rows, :] for ref in packed_refs], axis=0)
    listed = jnp.concatenate([x[:, :rows] for x in spare], axis=1)
    positive = jnp.concatenate([x[:, rows : 2 * rows] for x in spare], axis=1)
    return q, listed, positive


def load_kernel(q_hbm, listed_hbm, positive_hbm, weights_hbm, out_ref, weights_ref, ints, sems):
    rows, dim = q_hbm.shape
    fanout = listed_hbm.shape[0]
    copies = [
        pltpu.make_async_copy(q_hbm, out_ref.at[pl.ds(0, rows), :], sems.at[0]),
        pltpu.make_async_copy(listed_hbm, ints.at[0], sems.at[1]),
        pltpu.make_async_copy(positive_hbm, ints.at[1], sems.at[2]),
        pltpu.make_async_copy(weights_hbm, weights_ref, sems.at[3]),
    ]
    for copy in copies:
        copy.start()
    copies[1].wait()
    copies[2].wait()
    parts = [ints[0], ints[1]]
    if dim > 2 * rows:
        parts.append(jnp.zeros((fanout, dim - 2 * rows), jnp.int32))
    spare = jnp.concatenate(parts, axis=1)
    out_ref[rows:, :] = spare.astype(jnp.float32).astype(jnp.bfloat16)
    copies[0].wait()
    copies[3].wait()


def load_work(queries, listed, positive, weights):
    (rows, dim), fanout = queries.shape, listed.shape[0]
    vmem, hbm = pl.BlockSpec(memory_space=pltpu.VMEM), pl.BlockSpec(memory_space=pltpu.HBM)
    return pl.pallas_call(
        load_kernel,
        out_shape=(
            jax.ShapeDtypeStruct((rows + fanout, dim), queries.dtype),
            jax.ShapeDtypeStruct(weights.shape, weights.dtype),
        ),
        in_specs=[hbm] * 4,
        out_specs=(vmem, vmem),
        scratch_shapes=[
            pltpu.VMEM((2, fanout, rows), jnp.int32),
            pltpu.SemaphoreType.DMA((4,)),
        ],
        compiler_params=pltpu.CompilerParams(vmem_limit_bytes=KERNEL_VMEM),
        name="load",
    )(*(pltpu.with_memory_space_constraint(x, pltpu.HBM) for x in (queries, listed, positive, weights)))


def own_kernel(rows, base_ref, *refs):
    packed_refs, weight_refs = refs[: NEAR - 1], refs[NEAR - 1 : 2 * NEAR - 1]
    coef_ref, out_refs = refs[2 * NEAR - 1], refs[2 * NEAR :]
    labels = weight_refs[0].shape[0]
    q, listed, positive = unpack(packed_refs, rows)
    total = jnp.zeros(q.shape, jnp.float32)
    for j in range(NEAR):
        w = weight_refs[j][...]
        cluster = jnp.bitwise_xor(base_ref[0], j).astype(jnp.float32)
        coef = coefficients(w, q, listed, positive, cluster)
        coef_ref[j * labels : (j + 1) * labels, :] = coef
        total = total + tn_dot(coef, w)
    for s, out_ref in enumerate(out_refs):
        out_ref[...] = total[s * rows : (s + 1) * rows].astype(out_ref.dtype)


def grad_kernel(rows, base_ref, first_coef_ref, *refs):
    packed_refs, weight_refs = refs[:NEAR], refs[NEAR : 2 * NEAR]
    coef_ref, send_ref, own_ref, beside_ref = refs[2 * NEAR :]
    labels = weight_refs[0].shape[0]
    q, listed, positive = unpack(packed_refs[NEAR - 1 :], rows)
    all_q = jnp.concatenate([ref[:rows, :] for ref in packed_refs], axis=0)

    def part(j):
        cluster = jnp.bitwise_xor(base_ref[0], j).astype(jnp.float32)
        coef = coefficients(weight_refs[j][...], q, listed, positive, cluster)
        spot = slice(j * labels, (j + 1) * labels)
        coef_ref[spot, :] = coef
        all_coef = jnp.concatenate([first_coef_ref[spot, :], coef], axis=1)
        return jnp.dot(all_coef, all_q, preferred_element_type=jnp.float32)

    send_ref[:labels, :] = part(1).astype(jnp.bfloat16)
    send_ref[labels:, :] = part(3).astype(jnp.bfloat16)
    own_ref[...] = part(0)
    beside_ref[...] = part(2)


def back_kernel(base_ref, coef_ref, *refs):
    weight_refs, out_ref = refs[:NEAR], refs[NEAR]
    labels = weight_refs[0].shape[0]
    total = jnp.zeros(out_ref.shape, jnp.float32)
    for j in range(NEAR):
        total = total + tn_dot(coef_ref[j * labels : (j + 1) * labels, :], weight_refs[j][...])
    out_ref[...] = total.astype(out_ref.dtype)


def near_device(queries, shortlist, positives, weights, first_moment, second_moment):
    owners = lax.axis_size("cluster")
    rows = shortlist.shape[0]
    labels, dim = weights.shape[1:]
    base = lax.axis_index("cluster").astype(jnp.int32).reshape(1)
    low_type, wide = jnp.bfloat16, jnp.float32
    cut = labels * 5 // 8 // 16 * 16

    def over_cluster(x, bits):
        return lax.ppermute(x, "cluster", [(i, i ^ bits) for i in range(owners)])

    def over_dp(x):
        return lax.ppermute(x, "dp", [(0, 1), (1, 0)])

    packed, own_weights = load_work(queries, shortlist.T, positives.T, weights[0])
    q1 = over_cluster(packed, NEAR)
    q2 = over_cluster(packed, 2 * NEAR)
    packs = [packed, q1, q2, over_cluster(q2, NEAR)]
    weight_core = over_cluster(own_weights, 1)
    beside = over_cluster(own_weights, 2)
    near_weights = [own_weights, weight_core, beside, over_cluster(beside, 1)]

    flops = 2 * rows * NEAR * labels * dim
    block = ((rows, dim), low_type)
    first_coef, total, *backs = kernel_call(
        functools.partial(own_kernel, rows),
        [((NEAR * labels, 3 * rows), low_type), ((rows, dim), wide), block, block],
        [base, *packs[:3], *near_weights],
        6 * flops,
    )
    coef, send, own, near = kernel_call(
        functools.partial(grad_kernel, rows),
        [
            ((NEAR * labels, rows), low_type),
            ((2 * labels, dim), low_type),
            ((labels, dim), wide),
            ((labels, dim), wide),
        ],
        [base, first_coef, *packs, *near_weights],
        5 * flops,
    )
    got = over_cluster(send, 1).astype(wide)
    backs += kernel_call(back_kernel, [block], [base, coef, *near_weights], flops)
    for s, back in enumerate(backs, 1):
        total = total + over_cluster(back, s * NEAR).astype(wide)
    query_grad = total.astype(low_type)

    own = own + got[:labels]
    near = near + got[labels:]
    low = jnp.concatenate([own[cut:], near[cut:]], axis=0).astype(low_type)
    got_top = over_cluster(near[:cut].astype(low_type), 2).astype(wide)
    got_low = over_dp(low).astype(wide)
    top = (own[:cut] + got_top).astype(low_type)
    low = low.astype(wide) + got_low
    low_own, low_near = low[: labels - cut], low[labels - cut :].astype(low_type)
    top = top.astype(wide) + over_dp(top).astype(wide)
    low_own = low_own + over_cluster(low_near, 2).astype(wide)
    gradient = lax.optimization_barrier(jnp.concatenate([top, low_own], axis=0))
    new_weights, new_first, new_second = adam_update(
        own_weights, first_moment[0], second_moment[0], gradient
    )
    return (new_weights[None], new_first[None], new_second[None], query_grad)


def owner_work(arrived_rows, arrived_labels, cluster_rows):
    label_ids = jnp.arange(cluster_rows.shape[0], dtype=jnp.int32)
    scores = lax.dot_general(
        arrived_rows, cluster_rows, (((1,), (1,)), ((), ())), preferred_element_type=jnp.float32
    )
    target = (arrived_labels[:, None] == label_ids[None, :]).astype(jnp.float32)
    coefficient = (jax.nn.sigmoid(scores) - target).astype(jnp.bfloat16)
    gradient = lax.dot_general(
        coefficient, arrived_rows, (((0,), (0,)), ((), ())), preferred_element_type=jnp.float32
    )
    visit_grad = jnp.dot(coefficient, cluster_rows, preferred_element_type=jnp.float32).astype(
        jnp.bfloat16
    )
    return (gradient, visit_grad)


def dispatch_device(queries, shortlist, positives, weights, first_moment, second_moment):
    owners = lax.axis_size("cluster")
    rows_dev, fanout = shortlist.shape
    feature_dim = queries.shape[1]
    capacity = min(rows_dev, 2 * rows_dev * fanout // owners)
    visits = shortlist.reshape(-1)
    labels = positives.reshape(-1)
    onehot = (visits[:, None] == jnp.arange(owners, dtype=jnp.int32)[None, :]).astype(jnp.int32)
    visit_rank = jnp.sum((jnp.cumsum(onehot, axis=0) - onehot) * onehot, axis=1)
    slot_index = visits * capacity + visit_rank
    slot_visit = (
        jnp.full((owners * capacity,), -1, jnp.int32)
        .at[slot_index]
        .set(jnp.arange(visits.shape[0], dtype=jnp.int32))
    )
    filled = slot_visit >= 0
    clamped = jnp.maximum(slot_visit, 0)
    send_rows = jnp.where(filled[:, None], queries[clamped // fanout], jnp.zeros((), queries.dtype))
    send_labels = jnp.where(filled, labels[clamped], -1)
    cluster_rows = weights[0]
    exchange = functools.partial(
        lax.all_to_all, axis_name="cluster", split_axis=0, concat_axis=0, tiled=True
    )
    arrived_rows = exchange(send_rows.reshape(owners, capacity, feature_dim))
    arrived_labels = exchange(send_labels.reshape(owners, capacity))
    gradient, visit_grad = owner_work(
        arrived_rows.reshape(-1, feature_dim), arrived_labels.reshape(-1), cluster_rows
    )
    returned = exchange(visit_grad.reshape(owners, capacity, feature_dim))
    per_visit = returned.reshape(-1, feature_dim)[slot_index].astype(jnp.float32)
    query_grad = jnp.sum(per_visit.reshape(rows_dev, fanout, feature_dim), axis=1).astype(
        jnp.bfloat16
    )
    summed = lax.psum(gradient.astype(jnp.bfloat16), "dp").astype(jnp.float32)
    new_weights, new_first, new_second = adam_update(
        cluster_rows, first_moment[0], second_moment[0], summed
    )
    return (new_weights[None], new_first[None], new_second[None], query_grad)


def on_device(queries, shortlist, *rest):
    owners, copies = lax.axis_size("cluster"), lax.axis_size("dp")
    rows_dev, fanout = shortlist.shape
    dense = 2 * fanout >= owners and owners == NEAR * NEAR and copies == 2
    dense = dense and rest[1].shape[1] <= 256 and queries.shape[1] >= 2 * rows_dev
    step = near_device if dense else dispatch_device
    return step(queries, shortlist, *rest)


def solution(mesh):
    split = P(("dp", "cluster"), None)
    owned = P("cluster", None, None)
    return jax.shard_map(
        on_device,
        mesh=mesh,
        in_specs=(split, split, split, owned, owned, owned),
        out_specs=(owned, owned, owned, split),
        check_vma=False,
    )
```

```python
import functools

import jax
import jax.numpy as jnp
from jax import lax
from jax.experimental import pallas as pl
from jax.experimental.pallas import tpu as pltpu
from jax.sharding import PartitionSpec as P


beta_one = 0.9
beta_two = 0.999
learn_rate = 0.01
adam_eps = 1e-08
adam_step = 10.0

NEAR = 4
KERNEL_VMEM = 16 << 20
PIECE = 48


def adam_update(cluster_weights, first_moment, second_moment, gradient):
    first_new = beta_one * first_moment + (1.0 - beta_one) * gradient
    second_new = beta_two * second_moment + (1.0 - beta_two) * gradient * gradient
    first_hat = first_new / (1.0 - beta_one**adam_step)
    second_hat = second_new / (1.0 - beta_two**adam_step)
    stepped = cluster_weights.astype(jnp.float32) - learn_rate * first_hat / (
        jnp.sqrt(second_hat) + adam_eps
    )
    return (stepped.astype(jnp.bfloat16), first_new, second_new)


def tn_dot(a, b):
    return lax.dot_general(a, b, (((0,), (0,)), ((), ())), preferred_element_type=jnp.float32)


def nt_dot(a, b):
    return lax.dot_general(a, b, (((1,), (1,)), ((), ())), preferred_element_type=jnp.float32)


def kernel_call(kernel, outs, args, flops, far=0):
    vmem, hbm = pl.BlockSpec(memory_space=pltpu.VMEM), pl.BlockSpec(memory_space=pltpu.HBM)
    specs = [pl.BlockSpec(memory_space=pltpu.SMEM)] + [hbm] * far + [vmem] * (len(args) - 1 - far)
    args = [
        pltpu.with_memory_space_constraint(x, pltpu.HBM) if spec is hbm else x
        for x, spec in zip(args, specs)
    ]
    return pl.pallas_call(
        kernel,
        out_shape=tuple(jax.ShapeDtypeStruct(shape, kind) for shape, kind in outs),
        in_specs=specs,
        out_specs=tuple([vmem] * len(outs)),
        scratch_shapes=[pltpu.SemaphoreType.DMA((far,))] if far else [],
        compiler_params=pltpu.CompilerParams(vmem_limit_bytes=KERNEL_VMEM),
        cost_estimate=pl.CostEstimate(flops=flops, bytes_accessed=1 << 20, transcendentals=0),
    )(*args)


def coefficients(weights, q, listed, positive, cluster):
    labels, rows = weights.shape[0], q.shape[0]
    code = jnp.max(jnp.where(listed == cluster, positive, -1.0), axis=0, keepdims=True)
    label_ids = lax.broadcasted_iota(jnp.int32, (labels, rows), 0)
    target = (label_ids == code.astype(jnp.int32)).astype(jnp.float32)
    coef = jax.nn.sigmoid(nt_dot(weights, q)) - target
    return jnp.where(code >= 0.0, coef, 0.0).astype(jnp.bfloat16)


def unpack(packed_refs, rows):
    spare = [ref[rows:, :].astype(jnp.float32) for ref in packed_refs]
    q = jnp.concatenate([ref[:rows, :] for ref in packed_refs], axis=0)
    listed = jnp.concatenate([x[:, :rows] for x in spare], axis=1)
    positive = jnp.concatenate([x[:, rows : 2 * rows] for x in spare], axis=1)
    return q, listed, positive


def load_kernel(q_hbm, listed_hbm, positive_hbm, weights_hbm, out_ref, weights_ref, ints, sems):
    rows, dim = q_hbm.shape
    fanout = listed_hbm.shape[0]
    copies = [
        pltpu.make_async_copy(q_hbm, out_ref.at[pl.ds(0, rows), :], sems.at[0]),
        pltpu.make_async_copy(listed_hbm, ints.at[0], sems.at[1]),
        pltpu.make_async_copy(positive_hbm, ints.at[1], sems.at[2]),
        pltpu.make_async_copy(weights_hbm, weights_ref, sems.at[3]),
    ]
    for copy in copies:
        copy.start()
    copies[1].wait()
    copies[2].wait()
    parts = [ints[0], ints[1]]
    if dim > 2 * rows:
        parts.append(jnp.zeros((fanout, dim - 2 * rows), jnp.int32))
    spare = jnp.concatenate(parts, axis=1)
    out_ref[rows:, :] = spare.astype(jnp.float32).astype(jnp.bfloat16)
    copies[0].wait()
    copies[3].wait()


def load_work(queries, listed, positive, weights):
    (rows, dim), fanout = queries.shape, listed.shape[0]
    vmem, hbm = pl.BlockSpec(memory_space=pltpu.VMEM), pl.BlockSpec(memory_space=pltpu.HBM)
    return pl.pallas_call(
        load_kernel,
        out_shape=(
            jax.ShapeDtypeStruct((rows + fanout, dim), queries.dtype),
            jax.ShapeDtypeStruct(weights.shape, weights.dtype),
        ),
        in_specs=[hbm] * 4,
        out_specs=(vmem, vmem),
        scratch_shapes=[
            pltpu.VMEM((2, fanout, rows), jnp.int32),
            pltpu.SemaphoreType.DMA((4,)),
        ],
        compiler_params=pltpu.CompilerParams(vmem_limit_bytes=KERNEL_VMEM),
        name="load",
    )(*(pltpu.with_memory_space_constraint(x, pltpu.HBM) for x in (queries, listed, positive, weights)))


def own_kernel(rows, near, base_ref, *refs):
    blocks = NEAR - 1
    packed_refs, weight_refs = refs[:blocks], refs[blocks : blocks + len(near)]
    so_far_ref, coef_ref, out_refs = None, refs[blocks + len(near)], refs[blocks + len(near) + 1 :]
    if len(out_refs) > 1:
        so_far_ref, coef_ref, out_refs = coef_ref, out_refs[0], out_refs[1:]
    labels = weight_refs[0].shape[0]
    q, listed, positive = unpack(packed_refs, rows)
    total = jnp.zeros(q.shape, jnp.float32) if so_far_ref is None else so_far_ref[...]
    for at, j in enumerate(near):
        w = weight_refs[at][...]
        cluster = jnp.bitwise_xor(base_ref[0], j).astype(jnp.float32)
        coef = coefficients(w, q, listed, positive, cluster)
        coef_ref[at * labels : (at + 1) * labels, :] = coef
        total = total + tn_dot(coef, w)
    if len(out_refs) == 1:
        out_refs[0][...] = total
        return
    for s, out_ref in enumerate(out_refs):
        out_ref[...] = total[s * rows : (s + 1) * rows].astype(out_ref.dtype)


def first_kernel(rows, base_ref, first_hbm, second_hbm, *refs):
    *work, first_ref, second_ref, sems = refs
    copies = [
        pltpu.make_async_copy(first_hbm, first_ref, sems.at[0]),
        pltpu.make_async_copy(second_hbm, second_ref, sems.at[1]),
    ]
    for copy in copies:
        copy.start()
    own_kernel(rows, (0, 1), base_ref, *work)
    for copy in copies:
        copy.wait()


def grad_part(rows, j, base_ref, weight_ref, first_coef, packed_refs):
    q, listed, positive = unpack(packed_refs[NEAR - 1 :], rows)
    all_q = jnp.concatenate([ref[:rows, :] for ref in packed_refs], axis=0)
    cluster = jnp.bitwise_xor(base_ref[0], j).astype(jnp.float32)
    coef = coefficients(weight_ref[...], q, listed, positive, cluster)
    all_coef = jnp.concatenate([first_coef, coef], axis=1)
    return coef, jnp.dot(all_coef, all_q, preferred_element_type=jnp.float32)


def sent_kernel(rows, labels, base_ref, far_coef_ref, weight_ref, *refs):
    packed_refs, (coef_ref, send_ref) = refs[:NEAR], refs[NEAR:]
    coef_ref[...], part = grad_part(
        rows, 3, base_ref, weight_ref, far_coef_ref[labels:, :], packed_refs
    )
    send_ref[...] = part.astype(send_ref.dtype)


def middle_kernel(rows, labels, base_ref, near_coef_ref, far_coef_ref, *refs):
    (weight1_ref, weight2_ref), packed_refs = refs[:2], refs[2 : NEAR + 2]
    coef1_ref, coef2_ref, send_ref, beside_ref = refs[NEAR + 2 :]
    coef1_ref[...], part = grad_part(
        rows, 1, base_ref, weight1_ref, near_coef_ref[labels:, :], packed_refs
    )
    send_ref[...] = part.astype(send_ref.dtype)
    coef2_ref[...], beside_ref[...] = grad_part(
        rows, 2, base_ref, weight2_ref, far_coef_ref[:labels, :], packed_refs
    )


def last_kernel(rows, labels, base_ref, near_coef_ref, *refs):
    coef_refs, weight_refs = refs[: NEAR - 1], refs[NEAR - 1 : 2 * NEAR - 1]
    packed_refs, (own_ref, back_ref) = refs[2 * NEAR - 1 : 3 * NEAR - 1], refs[3 * NEAR - 1 :]
    coef, own_ref[...] = grad_part(
        rows, 0, base_ref, weight_refs[0], near_coef_ref[:labels, :], packed_refs
    )
    total = tn_dot(coef, weight_refs[0][...])
    for coef_ref, weight_ref in zip(coef_refs, weight_refs[1:]):
        total = total + tn_dot(coef_ref[...], weight_ref[...])
    back_ref[...] = total.astype(back_ref.dtype)


def sum_kernel(base_ref, mine_ref, got_ref, out_ref):
    out_ref[...] = (mine_ref[...] + got_ref[...].astype(jnp.float32)).astype(out_ref.dtype)


def beside_kernel(base_ref, mine_ref, got_ref, top_ref, low_ref):
    cut = top_ref.shape[0]
    total = mine_ref[...] + got_ref[...].astype(jnp.float32)
    top_ref[...] = total[:cut].astype(top_ref.dtype)
    low_ref[...] = total[cut:].astype(low_ref.dtype)


def mine_kernel(base_ref, mine_ref, got_ref, low_beside_ref, top_ref, low_ref):
    cut = top_ref.shape[0]
    rest = low_beside_ref.shape[0]
    total = mine_ref[...] + got_ref[...].astype(jnp.float32)
    top_ref[...] = total[:cut]
    low_ref[:rest, :] = total[cut:].astype(low_ref.dtype)
    low_ref[rest:, :] = low_beside_ref[...]


def adam_kernel(start, pieces, mine_ref, got_ref, weights_ref, first_ref, second_ref, *refs):
    *outs, sems = refs[-7:]
    outs_hbm, scratch = outs[:3], outs[3:]
    copies, at = [], 0
    for piece, rows in enumerate(pieces):
        here, there = slice(at, at + rows), slice(start + at, start + at + rows)
        gradient = mine_ref[here, :].astype(jnp.float32) + got_ref[here, :].astype(jnp.float32)
        new = adam_update(
            weights_ref[there, :], first_ref[there, :], second_ref[there, :], gradient
        )
        for which, value in enumerate(new):
            scratch[which][here, :] = value
            copies.append(
                pltpu.make_async_copy(
                    scratch[which].at[pl.ds(at, rows), :],
                    outs_hbm[which].at[pl.ds(start + at, rows), :],
                    sems.at[which, piece],
                )
            )
            copies[-1].start()
        at += rows
    for copy in copies:
        copy.wait()


def adam_work(start, mine, got, old, earlier):
    rows, dim = mine.shape
    pieces = [min(PIECE, rows - at) for at in range(0, rows, PIECE)]
    vmem, hbm = pl.BlockSpec(memory_space=pltpu.VMEM), pl.BlockSpec(memory_space=pltpu.HBM)
    earlier = [pltpu.with_memory_space_constraint(x, pltpu.HBM) for x in earlier]
    return pl.pallas_call(
        functools.partial(adam_kernel, start, pieces),
        out_shape=tuple(pltpu.HBM(x.shape, x.dtype) for x in old),
        in_specs=[vmem] * 5 + [hbm] * len(earlier),
        out_specs=(hbm, hbm, hbm),
        scratch_shapes=[pltpu.VMEM((rows, dim), x.dtype) for x in old]
        + [pltpu.SemaphoreType.DMA((3, len(pieces)))],
        input_output_aliases={5 + i: i for i in range(len(earlier))},
        compiler_params=pltpu.CompilerParams(vmem_limit_bytes=KERNEL_VMEM),
        cost_estimate=pl.CostEstimate(
            flops=20 * rows * dim, bytes_accessed=20 * rows * dim, transcendentals=rows * dim
        ),
    )(mine, got, *old, *earlier)


def near_device(queries, shortlist, positives, weights, first_moment, second_moment):
    owners = lax.axis_size("cluster")
    rows = shortlist.shape[0]
    labels, dim = weights.shape[1:]
    base = lax.axis_index("cluster").astype(jnp.int32).reshape(1)
    low_type, wide = jnp.bfloat16, jnp.float32
    cut = labels * 11 // 16 // 16 * 16

    def over_cluster(x, bits):
        return lax.ppermute(x, "cluster", [(i, i ^ bits) for i in range(owners)])

    def over_dp(x):
        return lax.ppermute(x, "dp", [(0, 1), (1, 0)])

    packed, own_weights = load_work(queries, shortlist.T, positives.T, weights[0])
    q1 = over_cluster(packed, NEAR)
    q2 = over_cluster(packed, 2 * NEAR)
    packs = [packed, q1, q2, over_cluster(q2, NEAR)]
    weight_core = over_cluster(own_weights, 1)
    beside = over_cluster(own_weights, 2)
    near_weights = [own_weights, weight_core, beside, over_cluster(beside, 1)]

    flops = 2 * rows * labels * dim
    block, coefs = ((rows, dim), low_type), ((2 * labels, 3 * rows), low_type)
    moment = ((labels, dim), wide)
    near_coef, so_far, old_first, old_second = kernel_call(
        functools.partial(first_kernel, rows),
        [coefs, ((3 * rows, dim), wide), moment, moment],
        [base, first_moment[0], second_moment[0], *packs[:3], *near_weights[:2]],
        12 * flops,
        far=2,
    )
    far_coef, total, *backs = kernel_call(
        functools.partial(own_kernel, rows, (2, 3)),
        [coefs, ((rows, dim), wide), block, block],
        [base, *packs[:3], *near_weights[2:], so_far],
        12 * flops,
    )
    last_coef, part = ((labels, rows), low_type), ((labels, dim), low_type)
    kernel = lambda body, outs, args, times: kernel_call(
        functools.partial(body, rows, labels), outs, [base, *args], times * flops
    )
    coef3, send3 = kernel(sent_kernel, [last_coef, part], [far_coef, near_weights[3], *packs], 5)
    got3 = over_cluster(send3, 1)
    coef1, coef2, send1, near = kernel(
        middle_kernel,
        [last_coef, last_coef, part, ((labels, dim), wide)],
        [near_coef, far_coef, *near_weights[1:3], *packs],
        10,
    )
    got1 = over_cluster(send1, 1)
    top_near, low_near = kernel_call(
        beside_kernel,
        [((cut, dim), low_type), ((labels - cut, dim), low_type)],
        [base, near, got3],
        labels * dim,
    )
    got_top = over_cluster(top_near, 2)
    own, back = kernel(
        last_kernel,
        [((labels, dim), wide), block],
        [near_coef, coef1, coef2, coef3, *near_weights, *packs],
        9,
    )
    backs.append(back)
    own_top, low = kernel_call(
        mine_kernel,
        [((cut, dim), wide), ((2 * (labels - cut), dim), low_type)],
        [base, own, got1, low_near],
        labels * dim,
    )
    got_low = over_dp(low).astype(wide)
    for s, back in enumerate(backs, 1):
        total = total + over_cluster(back, s * NEAR).astype(wide)
    query_grad = total.astype(low_type)

    (top,) = kernel_call(sum_kernel, [((cut, dim), low_type)], [base, own_top, got_top], cut * dim)
    low = low.astype(wide) + got_low
    low_own, low_near = low[: labels - cut], low[labels - cut :].astype(low_type)
    got_top, got_low = over_dp(top), over_cluster(low_near, 2)
    old = (own_weights, old_first, old_second)
    partly = adam_work(cut, low_own, got_low, old, ())
    new_weights, new_first, new_second = adam_work(0, top, got_top, old, partly)
    return (new_weights[None], new_first[None], new_second[None], query_grad)


def owner_work(arrived_rows, arrived_labels, cluster_rows):
    label_ids = jnp.arange(cluster_rows.shape[0], dtype=jnp.int32)
    scores = lax.dot_general(
        arrived_rows, cluster_rows, (((1,), (1,)), ((), ())), preferred_element_type=jnp.float32
    )
    target = (arrived_labels[:, None] == label_ids[None, :]).astype(jnp.float32)
    coefficient = (jax.nn.sigmoid(scores) - target).astype(jnp.bfloat16)
    gradient = lax.dot_general(
        coefficient, arrived_rows, (((0,), (0,)), ((), ())), preferred_element_type=jnp.float32
    )
    visit_grad = jnp.dot(coefficient, cluster_rows, preferred_element_type=jnp.float32).astype(
        jnp.bfloat16
    )
    return (gradient, visit_grad)


def dispatch_device(queries, shortlist, positives, weights, first_moment, second_moment):
    owners = lax.axis_size("cluster")
    rows_dev, fanout = shortlist.shape
    feature_dim = queries.shape[1]
    capacity = min(rows_dev, 2 * rows_dev * fanout // owners)
    visits = shortlist.reshape(-1)
    labels = positives.reshape(-1)
    onehot = (visits[:, None] == jnp.arange(owners, dtype=jnp.int32)[None, :]).astype(jnp.int32)
    visit_rank = jnp.sum((jnp.cumsum(onehot, axis=0) - onehot) * onehot, axis=1)
    slot_index = visits * capacity + visit_rank
    slot_visit = (
        jnp.full((owners * capacity,), -1, jnp.int32)
        .at[slot_index]
        .set(jnp.arange(visits.shape[0], dtype=jnp.int32))
    )
    filled = slot_visit >= 0
    clamped = jnp.maximum(slot_visit, 0)
    send_rows = jnp.where(filled[:, None], queries[clamped // fanout], jnp.zeros((), queries.dtype))
    send_labels = jnp.where(filled, labels[clamped], -1)
    cluster_rows = weights[0]
    exchange = functools.partial(
        lax.all_to_all, axis_name="cluster", split_axis=0, concat_axis=0, tiled=True
    )
    arrived_rows = exchange(send_rows.reshape(owners, capacity, feature_dim))
    arrived_labels = exchange(send_labels.reshape(owners, capacity))
    gradient, visit_grad = owner_work(
        arrived_rows.reshape(-1, feature_dim), arrived_labels.reshape(-1), cluster_rows
    )
    returned = exchange(visit_grad.reshape(owners, capacity, feature_dim))
    per_visit = returned.reshape(-1, feature_dim)[slot_index].astype(jnp.float32)
    query_grad = jnp.sum(per_visit.reshape(rows_dev, fanout, feature_dim), axis=1).astype(
        jnp.bfloat16
    )
    summed = lax.psum(gradient.astype(jnp.bfloat16), "dp").astype(jnp.float32)
    new_weights, new_first, new_second = adam_update(
        cluster_rows, first_moment[0], second_moment[0], summed
    )
    return (new_weights[None], new_first[None], new_second[None], query_grad)


def on_device(queries, shortlist, *rest):
    owners, copies = lax.axis_size("cluster"), lax.axis_size("dp")
    rows_dev, fanout = shortlist.shape
    dense = 2 * fanout >= owners and owners == NEAR * NEAR and copies == 2
    dense = dense and rest[1].shape[1] <= 256 and queries.shape[1] >= 2 * rows_dev
    step = near_device if dense else dispatch_device
    return step(queries, shortlist, *rest)


def solution(mesh):
    split = P(("dp", "cluster"), None)
    owned = P("cluster", None, None)
    return jax.shard_map(
        on_device,
        mesh=mesh,
        in_specs=(split, split, split, owned, owned, owned),
        out_specs=(owned, owned, owned, split),
        check_vma=False,
    )
```

```python
import functools

import jax
import jax.numpy as jnp
from jax import lax
from jax.experimental import pallas as pl
from jax.experimental.pallas import tpu as pltpu
from jax.sharding import PartitionSpec as P


beta_one = 0.9
beta_two = 0.999
learn_rate = 0.01
adam_eps = 1e-08
adam_step = 10.0

NEAR = 4
KERNEL_VMEM = 16 << 20
PIECE = 48


def adam_update(cluster_weights, first_moment, second_moment, gradient):
    first_new = beta_one * first_moment + (1.0 - beta_one) * gradient
    second_new = beta_two * second_moment + (1.0 - beta_two) * gradient * gradient
    first_hat = first_new / (1.0 - beta_one**adam_step)
    second_hat = second_new / (1.0 - beta_two**adam_step)
    stepped = cluster_weights.astype(jnp.float32) - learn_rate * first_hat / (
        jnp.sqrt(second_hat) + adam_eps
    )
    return (stepped.astype(jnp.bfloat16), first_new, second_new)


def tn_dot(a, b):
    return lax.dot_general(a, b, (((0,), (0,)), ((), ())), preferred_element_type=jnp.float32)


def nt_dot(a, b):
    return lax.dot_general(a, b, (((1,), (1,)), ((), ())), preferred_element_type=jnp.float32)


def kernel_call(kernel, outs, args, flops, far=0):
    vmem, hbm = pl.BlockSpec(memory_space=pltpu.VMEM), pl.BlockSpec(memory_space=pltpu.HBM)
    specs = [pl.BlockSpec(memory_space=pltpu.SMEM)] + [hbm] * far + [vmem] * (len(args) - 1 - far)
    args = [
        pltpu.with_memory_space_constraint(x, pltpu.HBM) if spec is hbm else x
        for x, spec in zip(args, specs)
    ]
    return pl.pallas_call(
        kernel,
        out_shape=tuple(jax.ShapeDtypeStruct(shape, kind) for shape, kind in outs),
        in_specs=specs,
        out_specs=tuple([vmem] * len(outs)),
        scratch_shapes=[pltpu.SemaphoreType.DMA((far,))] if far else [],
        compiler_params=pltpu.CompilerParams(vmem_limit_bytes=KERNEL_VMEM),
        cost_estimate=pl.CostEstimate(flops=flops, bytes_accessed=1 << 20, transcendentals=0),
    )(*args)


def coefficients(weights, q, listed, positive, cluster):
    labels, rows = weights.shape[0], q.shape[0]
    code = jnp.max(jnp.where(listed == cluster, positive, -1.0), axis=0, keepdims=True)
    label_ids = lax.broadcasted_iota(jnp.int32, (labels, rows), 0)
    target = (label_ids == code.astype(jnp.int32)).astype(jnp.float32)
    coef = jax.nn.sigmoid(nt_dot(weights, q)) - target
    return jnp.where(code >= 0.0, coef, 0.0).astype(jnp.bfloat16)


def unpack(packed_refs, rows):
    spare = [ref[rows:, :].astype(jnp.float32) for ref in packed_refs]
    q = jnp.concatenate([ref[:rows, :] for ref in packed_refs], axis=0)
    listed = jnp.concatenate([x[:, :rows] for x in spare], axis=1)
    positive = jnp.concatenate([x[:, rows : 2 * rows] for x in spare], axis=1)
    return q, listed, positive


def load_kernel(q_hbm, listed_hbm, positive_hbm, weights_hbm, out_ref, weights_ref, ints, sems):
    rows, dim = q_hbm.shape
    fanout = listed_hbm.shape[0]
    copies = [
        pltpu.make_async_copy(q_hbm, out_ref.at[pl.ds(0, rows), :], sems.at[0]),
        pltpu.make_async_copy(listed_hbm, ints.at[0], sems.at[1]),
        pltpu.make_async_copy(positive_hbm, ints.at[1], sems.at[2]),
        pltpu.make_async_copy(weights_hbm, weights_ref, sems.at[3]),
    ]
    for copy in copies:
        copy.start()
    copies[1].wait()
    copies[2].wait()
    parts = [ints[0], ints[1]]
    if dim > 2 * rows:
        parts.append(jnp.zeros((fanout, dim - 2 * rows), jnp.int32))
    spare = jnp.concatenate(parts, axis=1)
    out_ref[rows:, :] = spare.astype(jnp.float32).astype(jnp.bfloat16)
    copies[0].wait()
    copies[3].wait()


def load_work(queries, listed, positive, weights):
    (rows, dim), fanout = queries.shape, listed.shape[0]
    vmem, hbm = pl.BlockSpec(memory_space=pltpu.VMEM), pl.BlockSpec(memory_space=pltpu.HBM)
    return pl.pallas_call(
        load_kernel,
        out_shape=(
            jax.ShapeDtypeStruct((rows + fanout, dim), queries.dtype),
            jax.ShapeDtypeStruct(weights.shape, weights.dtype),
        ),
        in_specs=[hbm] * 4,
        out_specs=(vmem, vmem),
        scratch_shapes=[
            pltpu.VMEM((2, fanout, rows), jnp.int32),
            pltpu.SemaphoreType.DMA((4,)),
        ],
        compiler_params=pltpu.CompilerParams(vmem_limit_bytes=KERNEL_VMEM),
        name="load",
    )(*(pltpu.with_memory_space_constraint(x, pltpu.HBM) for x in (queries, listed, positive, weights)))


def own_kernel(rows, near, base_ref, *refs):
    blocks = NEAR - 1
    packed_refs, weight_refs = refs[:blocks], refs[blocks : blocks + len(near)]
    so_far_ref, coef_ref, out_refs = None, refs[blocks + len(near)], refs[blocks + len(near) + 1 :]
    if len(out_refs) > 1:
        so_far_ref, coef_ref, out_refs = coef_ref, out_refs[0], out_refs[1:]
    labels = weight_refs[0].shape[0]
    q, listed, positive = unpack(packed_refs, rows)
    total = jnp.zeros(q.shape, jnp.float32) if so_far_ref is None else so_far_ref[...]
    for at, j in enumerate(near):
        w = weight_refs[at][...]
        cluster = jnp.bitwise_xor(base_ref[0], j).astype(jnp.float32)
        coef = coefficients(w, q, listed, positive, cluster)
        coef_ref[at * labels : (at + 1) * labels, :] = coef
        total = total + tn_dot(coef, w)
    if len(out_refs) == 1:
        out_refs[0][...] = total
        return
    for s, out_ref in enumerate(out_refs):
        out_ref[...] = total[s * rows : (s + 1) * rows].astype(out_ref.dtype)


def first_kernel(rows, base_ref, first_hbm, second_hbm, *refs):
    *work, first_ref, second_ref, sems = refs
    copies = [
        pltpu.make_async_copy(first_hbm, first_ref, sems.at[0]),
        pltpu.make_async_copy(second_hbm, second_ref, sems.at[1]),
    ]
    for copy in copies:
        copy.start()
    own_kernel(rows, (0, 1), base_ref, *work)
    for copy in copies:
        copy.wait()


def grad_part(rows, j, base_ref, weight_ref, first_coef, packed_refs):
    q, listed, positive = unpack(packed_refs[NEAR - 1 :], rows)
    all_q = jnp.concatenate([ref[:rows, :] for ref in packed_refs], axis=0)
    cluster = jnp.bitwise_xor(base_ref[0], j).astype(jnp.float32)
    coef = coefficients(weight_ref[...], q, listed, positive, cluster)
    all_coef = jnp.concatenate([first_coef, coef], axis=1)
    return coef, jnp.dot(all_coef, all_q, preferred_element_type=jnp.float32)


def sent_kernel(rows, labels, base_ref, far_coef_ref, weight_ref, *refs):
    packed_refs, (coef_ref, send_ref) = refs[:NEAR], refs[NEAR:]
    coef_ref[...], part = grad_part(
        rows, 3, base_ref, weight_ref, far_coef_ref[labels:, :], packed_refs
    )
    send_ref[...] = part.astype(send_ref.dtype)


def middle_kernel(rows, labels, base_ref, near_coef_ref, far_coef_ref, *refs):
    (weight1_ref, weight2_ref), packed_refs = refs[:2], refs[2 : NEAR + 2]
    coef1_ref, coef2_ref, send_ref, beside_ref = refs[NEAR + 2 :]
    coef1_ref[...], part = grad_part(
        rows, 1, base_ref, weight1_ref, near_coef_ref[labels:, :], packed_refs
    )
    send_ref[...] = part.astype(send_ref.dtype)
    coef2_ref[...], beside_ref[...] = grad_part(
        rows, 2, base_ref, weight2_ref, far_coef_ref[:labels, :], packed_refs
    )


def last_kernel(rows, labels, base_ref, near_coef_ref, weight_ref, *refs):
    packed_refs, (coef_ref, own_ref) = refs[:NEAR], refs[NEAR:]
    coef_ref[...], own_ref[...] = grad_part(
        rows, 0, base_ref, weight_ref, near_coef_ref[:labels, :], packed_refs
    )


def back_kernel(rows, labels, base_ref, *refs):
    coef_refs, weight_refs, back_ref = refs[:NEAR], refs[NEAR : 2 * NEAR], refs[-1]
    total = jnp.zeros(back_ref.shape, jnp.float32)
    for coef_ref, weight_ref in zip(coef_refs, weight_refs):
        total = total + tn_dot(coef_ref[...], weight_ref[...])
    back_ref[...] = total.astype(back_ref.dtype)


def sum_kernel(base_ref, mine_ref, got_ref, out_ref):
    out_ref[...] = (mine_ref[...] + got_ref[...].astype(jnp.float32)).astype(out_ref.dtype)


def beside_kernel(base_ref, mine_ref, got_ref, top_ref, low_ref):
    cut = top_ref.shape[0]
    total = mine_ref[...] + got_ref[...].astype(jnp.float32)
    top_ref[...] = total[:cut].astype(top_ref.dtype)
    low_ref[...] = total[cut:].astype(low_ref.dtype)


def mine_kernel(base_ref, mine_ref, got_ref, low_beside_ref, top_ref, low_ref):
    cut = top_ref.shape[0]
    rest = low_beside_ref.shape[0]
    total = mine_ref[...] + got_ref[...].astype(jnp.float32)
    top_ref[...] = total[:cut]
    low_ref[:rest, :] = total[cut:].astype(low_ref.dtype)
    low_ref[rest:, :] = low_beside_ref[...]


def adam_kernel(start, pieces, mine_ref, got_ref, weights_ref, first_ref, second_ref, *refs):
    outs_hbm, scratch, sems = refs[-7:-4], refs[-4:-1], refs[-1]
    copies, at = [], 0
    for piece, rows in enumerate(pieces):
        here, there = slice(at, at + rows), slice(start + at, start + at + rows)
        gradient = mine_ref[here, :].astype(jnp.float32) + got_ref[here, :].astype(jnp.float32)
        new = adam_update(
            weights_ref[there, :], first_ref[there, :], second_ref[there, :], gradient
        )
        for which, value in enumerate(new):
            scratch[which][here, :] = value
            copies.append(
                pltpu.make_async_copy(
                    scratch[which].at[pl.ds(at, rows), :],
                    outs_hbm[which].at[pl.ds(start + at, rows), :],
                    sems.at[which, piece],
                )
            )
            copies[-1].start()
        at += rows
    for copy in copies:
        copy.wait()


def end_kernel(pieces, mine_ref, got_ref, weights_ref, first_ref, second_ref, total_ref, *refs):
    back_refs, refs = refs[: NEAR - 1], refs[NEAR - 1 :]
    _, _, _, *outs, query_hbm = refs[:7]
    *scratch, sems, query_ref, query_sem = refs[7:]
    total = total_ref[...]
    for ref in back_refs:
        total = total + ref[...].astype(jnp.float32)
    query_ref[...] = total.astype(query_ref.dtype)
    copy = pltpu.make_async_copy(query_ref, query_hbm, query_sem.at[0])
    copy.start()
    adam_kernel(
        0, pieces, mine_ref, got_ref, weights_ref, first_ref, second_ref, *outs, *scratch, sems
    )
    copy.wait()


def adam_work(start, mine, got, old, earlier, queries=()):
    rows, dim = mine.shape
    pieces = [min(PIECE, rows - at) for at in range(0, rows, PIECE)]
    vmem, hbm = pl.BlockSpec(memory_space=pltpu.VMEM), pl.BlockSpec(memory_space=pltpu.HBM)
    earlier = [pltpu.with_memory_space_constraint(x, pltpu.HBM) for x in earlier]
    outs = [pltpu.HBM(x.shape, x.dtype) for x in old]
    scratch = [pltpu.VMEM((rows, dim), x.dtype) for x in old]
    scratch.append(pltpu.SemaphoreType.DMA((3, len(pieces))))
    body = functools.partial(adam_kernel, start, pieces)
    if queries:
        shape, kind = queries[0].shape, queries[1].dtype
        outs.append(pltpu.HBM(shape, kind))
        scratch += [pltpu.VMEM(shape, kind), pltpu.SemaphoreType.DMA((1,))]
        body = functools.partial(end_kernel, pieces)
    ahead = 5 + len(queries)
    return pl.pallas_call(
        body,
        out_shape=tuple(outs),
        in_specs=[vmem] * ahead + [hbm] * len(earlier),
        out_specs=tuple([hbm] * len(outs)),
        scratch_shapes=scratch,
        input_output_aliases={ahead + i: i for i in range(len(earlier))},
        compiler_params=pltpu.CompilerParams(vmem_limit_bytes=KERNEL_VMEM),
        cost_estimate=pl.CostEstimate(
            flops=20 * rows * dim, bytes_accessed=20 * rows * dim, transcendentals=rows * dim
        ),
    )(mine, got, *old, *queries, *earlier)


def near_device(queries, shortlist, positives, weights, first_moment, second_moment):
    owners = lax.axis_size("cluster")
    rows = shortlist.shape[0]
    labels, dim = weights.shape[1:]
    base = lax.axis_index("cluster").astype(jnp.int32).reshape(1)
    low_type, wide = jnp.bfloat16, jnp.float32
    cut = labels * 11 // 16 // 16 * 16

    def over_cluster(x, bits):
        return lax.ppermute(x, "cluster", [(i, i ^ bits) for i in range(owners)])

    def over_dp(x):
        return lax.ppermute(x, "dp", [(0, 1), (1, 0)])

    packed, own_weights = load_work(queries, shortlist.T, positives.T, weights[0])
    q1 = over_cluster(packed, NEAR)
    q2 = over_cluster(packed, 2 * NEAR)
    packs = [packed, q1, q2, over_cluster(q2, NEAR)]
    weight_core = over_cluster(own_weights, 1)
    beside = over_cluster(own_weights, 2)
    near_weights = [own_weights, weight_core, beside, over_cluster(beside, 1)]

    flops = 2 * rows * labels * dim
    block, coefs = ((rows, dim), low_type), ((2 * labels, 3 * rows), low_type)
    moment = ((labels, dim), wide)
    near_coef, so_far, old_first, old_second = kernel_call(
        functools.partial(first_kernel, rows),
        [coefs, ((3 * rows, dim), wide), moment, moment],
        [base, first_moment[0], second_moment[0], *packs[:3], *near_weights[:2]],
        12 * flops,
        far=2,
    )
    far_coef, total, *backs = kernel_call(
        functools.partial(own_kernel, rows, (2, 3)),
        [coefs, ((rows, dim), wide), block, block],
        [base, *packs[:3], *near_weights[2:], so_far],
        12 * flops,
    )
    last_coef, part = ((labels, rows), low_type), ((labels, dim), low_type)
    kernel = lambda body, outs, args, times: kernel_call(
        functools.partial(body, rows, labels), outs, [base, *args], times * flops
    )
    coef3, send3 = kernel(sent_kernel, [last_coef, part], [far_coef, near_weights[3], *packs], 5)
    got3 = over_cluster(send3, 1)
    coef1, coef2, send1, near = kernel(
        middle_kernel,
        [last_coef, last_coef, part, ((labels, dim), wide)],
        [near_coef, far_coef, *near_weights[1:3], *packs],
        10,
    )
    got1 = over_cluster(send1, 1)
    top_near, low_near = kernel_call(
        beside_kernel,
        [((cut, dim), low_type), ((labels - cut, dim), low_type)],
        [base, near, got3],
        labels * dim,
    )
    got_top = over_cluster(top_near, 2)
    coef0, own = kernel(
        last_kernel, [last_coef, ((labels, dim), wide)], [near_coef, near_weights[0], *packs], 5
    )
    (back,) = kernel(back_kernel, [block], [coef0, coef1, coef2, coef3, *near_weights], 4)
    backs.append(back)
    own_top, low = kernel_call(
        mine_kernel,
        [((cut, dim), wide), ((2 * (labels - cut), dim), low_type)],
        [base, own, got1, low_near],
        labels * dim,
    )
    got_low = over_dp(low).astype(wide)
    returned = [over_cluster(back, s * NEAR) for s, back in enumerate(backs, 1)]

    (top,) = kernel_call(sum_kernel, [((cut, dim), low_type)], [base, own_top, got_top], cut * dim)
    low = low.astype(wide) + got_low
    low_own, low_near = low[: labels - cut], low[labels - cut :].astype(low_type)
    got_top, got_low = over_dp(top), over_cluster(low_near, 2)
    old = (own_weights, old_first, old_second)
    partly = adam_work(cut, low_own, got_low, old, ())
    new_weights, new_first, new_second, query_grad = adam_work(
        0, top, got_top, old, partly, (total, *returned)
    )
    return (new_weights[None], new_first[None], new_second[None], query_grad)


def owner_work(arrived_rows, arrived_labels, cluster_rows):
    label_ids = jnp.arange(cluster_rows.shape[0], dtype=jnp.int32)
    scores = lax.dot_general(
        arrived_rows, cluster_rows, (((1,), (1,)), ((), ())), preferred_element_type=jnp.float32
    )
    target = (arrived_labels[:, None] == label_ids[None, :]).astype(jnp.float32)
    coefficient = (jax.nn.sigmoid(scores) - target).astype(jnp.bfloat16)
    gradient = lax.dot_general(
        coefficient, arrived_rows, (((0,), (0,)), ((), ())), preferred_element_type=jnp.float32
    )
    visit_grad = jnp.dot(coefficient, cluster_rows, preferred_element_type=jnp.float32).astype(
        jnp.bfloat16
    )
    return (gradient, visit_grad)


def dispatch_device(queries, shortlist, positives, weights, first_moment, second_moment):
    owners = lax.axis_size("cluster")
    rows_dev, fanout = shortlist.shape
    feature_dim = queries.shape[1]
    capacity = min(rows_dev, 2 * rows_dev * fanout // owners)
    visits = shortlist.reshape(-1)
    labels = positives.reshape(-1)
    onehot = (visits[:, None] == jnp.arange(owners, dtype=jnp.int32)[None, :]).astype(jnp.int32)
    visit_rank = jnp.sum((jnp.cumsum(onehot, axis=0) - onehot) * onehot, axis=1)
    slot_index = visits * capacity + visit_rank
    slot_visit = (
        jnp.full((owners * capacity,), -1, jnp.int32)
        .at[slot_index]
        .set(jnp.arange(visits.shape[0], dtype=jnp.int32))
    )
    filled = slot_visit >= 0
    clamped = jnp.maximum(slot_visit, 0)
    send_rows = jnp.where(filled[:, None], queries[clamped // fanout], jnp.zeros((), queries.dtype))
    send_labels = jnp.where(filled, labels[clamped], -1)
    cluster_rows = weights[0]
    exchange = functools.partial(
        lax.all_to_all, axis_name="cluster", split_axis=0, concat_axis=0, tiled=True
    )
    arrived_rows = exchange(send_rows.reshape(owners, capacity, feature_dim))
    arrived_labels = exchange(send_labels.reshape(owners, capacity))
    gradient, visit_grad = owner_work(
        arrived_rows.reshape(-1, feature_dim), arrived_labels.reshape(-1), cluster_rows
    )
    returned = exchange(visit_grad.reshape(owners, capacity, feature_dim))
    per_visit = returned.reshape(-1, feature_dim)[slot_index].astype(jnp.float32)
    query_grad = jnp.sum(per_visit.reshape(rows_dev, fanout, feature_dim), axis=1).astype(
        jnp.bfloat16
    )
    summed = lax.psum(gradient.astype(jnp.bfloat16), "dp").astype(jnp.float32)
    new_weights, new_first, new_second = adam_update(
        cluster_rows, first_moment[0], second_moment[0], summed
    )
    return (new_weights[None], new_first[None], new_second[None], query_grad)


def on_device(queries, shortlist, *rest):
    owners, copies = lax.axis_size("cluster"), lax.axis_size("dp")
    rows_dev, fanout = shortlist.shape
    dense = 2 * fanout >= owners and owners == NEAR * NEAR and copies == 2
    dense = dense and rest[1].shape[1] <= 256 and queries.shape[1] >= 2 * rows_dev
    step = near_device if dense else dispatch_device
    return step(queries, shortlist, *rest)


def solution(mesh):
    split = P(("dp", "cluster"), None)
    owned = P("cluster", None, None)
    return jax.shard_map(
        on_device,
        mesh=mesh,
        in_specs=(split, split, split, owned, owned, owned),
        out_specs=(owned, owned, owned, split),
        check_vma=False,
    )
```
